32 devices in a mesh: tenant: 4 (over x, core), fsdp: 8 (over z, y).
Axes of the slice: x: 2, y: 2, z: 4, core: 2. Of those that a mesh axis runs over, the one named last changes fastest.
Arguments:
- tokens: bfloat16 [16384, 8192], P(('tenant', 'fsdp')), may hold values from -6 to 6
- cotangent: bfloat16 [16384, 1024], P(('tenant', 'fsdp')), may hold values from -6 to 6
- value_weight: bfloat16 [8192, 1024], P('fsdp'), may hold values from -0.0625 to 0.0625
- adapters: float32 [64, 16, 9216], P('tenant', None, 'fsdp'), may hold values from -2.5 to 2.5
- first_moment: float32 [64, 16, 9216], P('tenant', None, 'fsdp'), may hold values from -4 to 4
- second_moment: float32 [64, 16, 9216], P('tenant', None, 'fsdp'), may hold values from 0.2 to 2
- tenant_home: int32 [64], replicated, may hold values from 0 to 63, as said below
- read_tenants: int32 [32, 4], replicated, may hold values from 0 to 63, as said below
- row_tenant: int32 [16384], P(('tenant', 'fsdp')), may hold values from 0 to 63, as said below
Outputs:
- values: bfloat16 [16384, 1024], P(('tenant', 'fsdp'))
- token_grad: bfloat16 [16384, 8192], P(('tenant', 'fsdp'))
- new_adapters: float32 [64, 16, 9216], P('tenant', None, 'fsdp')
- new_first: float32 [64, 16, 9216], P('tenant', None, 'fsdp')
- new_second: float32 [64, 16, 9216], P('tenant', None, 'fsdp')
- refreshed: bfloat16 [128, 16, 9216], P(('tenant', 'fsdp'))
The draws below stay inside these ranges and needn't reach their ends.
Inputs may be any that keep to these rules, and one draw needn't show every extreme that they name: `tenant_home`: a permutation: every slot holds exactly one tenant; slot h belongs to index h // 16 of tenant. `read_tenants`: in each row, entry k is a tenant whose slot lies in index k of tenant. `row_tenant`: every row's tenant is in the read list of its block, and every entry of a block's read list is the tenant of some row of that block.
All inputs are finite; a program needn't handle non-finite values.
Results may differ from the reference program's by a relative error of at most 0.0055.
Values may be sent and summed in bfloat16 or wider, within the bound.
A program may use at most 128 MiB of HBM per device.

```python
import math
import jax
import jax.numpy as jnp
from jax import lax

MODEL_WIDTH = 8192
KV = 1024
ADAPTER_RANK = 16
TOK_DEV = 512
SLOTS = 16
PER_OWNER = 1
W_AD = 9216
TENANTS = 64
READS = 4
ROWS = 16384
N_TENANT = 4
N_FSDP = 8


def layout(key):
    perm_key = jax.random.fold_in(key, 11)
    pick_key = jax.random.fold_in(key, 12)
    row_key = jax.random.fold_in(key, 13)
    device_count = N_TENANT * N_FSDP
    home_of = jax.random.permutation(perm_key, TENANTS).astype(jnp.int32)
    tenant_at = jnp.argsort(home_of, stable=True).astype(jnp.int32)
    pick_keys = jax.random.split(pick_key, device_count * N_TENANT)
    picks = jax.vmap(lambda sub_key: jax.random.permutation(sub_key, SLOTS)[:PER_OWNER])(pick_keys).astype(jnp.int32)
    owners = (jnp.arange(device_count * N_TENANT) % N_TENANT).astype(jnp.int32)
    home_pick = owners[:, None] * SLOTS + picks
    read_list = jnp.take(tenant_at, home_pick.reshape(-1), axis=0).reshape(device_count, READS).astype(jnp.int32)
    row_pick = jax.random.randint(row_key, (device_count, TOK_DEV), 0, READS).astype(jnp.int32)
    row_pick = row_pick.at[:, :READS].set(jnp.arange(READS, dtype=jnp.int32)[None, :])
    row_list = jnp.take_along_axis(read_list, row_pick, axis=1).reshape(-1).astype(jnp.int32)
    return (home_of, read_list, row_list)


def draw_tenant_home(key, part):
    return layout(key)[0]


def draw_read_tenants(key, part):
    return layout(key)[1]


def draw_row_tenant(key, part):
    return layout(key)[2]


def block_scale(key, shape, cuts, least, largest):
    def one(dim, shards_of):
        draws = jax.random.uniform(jax.random.fold_in(jax.random.fold_in(key, 6), dim), (shards_of,), jnp.float32, least / len(cuts), largest / len(cuts))
        return jnp.repeat(jnp.exp(draws), shape[dim] // shards_of).reshape((-1,) + (1,) * (len(shape) - dim - 1))

    loudness = one(*cuts[0])
    for cut in cuts[1:]:
        loudness = loudness * one(*cut)
    return loudness


def gaussian(rng, dims, spread, bound, cuts=(), kind=jnp.bfloat16):
    factor_of = block_scale(rng, dims, cuts, -0.22, 0.18) if cuts else 1.0
    result = jax.random.normal(rng, dims, jnp.float32) * spread * factor_of
    return jnp.minimum(jnp.maximum(result, -bound), bound).astype(kind)


def setup_inputs(seed: int = 0) -> dict:
    key_of = jax.random.split(jax.random.key(seed), 10)
    return {
        "tokens": gaussian(key_of[0], (ROWS, MODEL_WIDTH), 1.0, 6.0, ((0, 32),)),
        "cotangent": gaussian(key_of[1], (ROWS, KV), 1.0, 6.0, ((0, 32),)),
        "value_weight": gaussian(key_of[2], (MODEL_WIDTH, KV), MODEL_WIDTH ** -0.5, 0.0625, ((0, 8),)),
        "adapters": gaussian(key_of[3], (TENANTS, ADAPTER_RANK, W_AD), 0.5, 2.5, ((0, 4), (2, 8)), jnp.float32),
        "first_moment": gaussian(key_of[4], (TENANTS, ADAPTER_RANK, W_AD), 1.0, 4.0, ((0, 4), (2, 8)), jnp.float32),
        "second_moment": jnp.clip(jnp.exp(math.log(2.0) - 2.3025851 * jax.random.uniform(key_of[5], (TENANTS, ADAPTER_RANK, W_AD), jnp.float32) ** block_scale(key_of[5], (TENANTS, ADAPTER_RANK, W_AD), ((0, 4), (2, 8)), -0.2, 0.2)), 0.2, 2.0),
        "tenant_home": draw_tenant_home(jax.random.fold_in(key_of[9], 71), 0),
        "read_tenants": draw_read_tenants(jax.random.fold_in(key_of[9], 71), 0),
        "row_tenant": draw_row_tenant(jax.random.fold_in(key_of[9], 71), 0),
    }


beta_first = 0.9
beta_second = 0.95
learn_rate = 0.1
adam_eps = 1e-08
corr_first = 1.0 - 0.9 ** 10
corr_second = 1.0 - 0.95 ** 10

def reference(tokens, cotangent, value_weight, adapters, first_moment, second_moment, tenant_home, read_tenants, row_tenant):
    device_count = N_TENANT * N_FSDP
    adapter_scale = 2.0 / math.sqrt(MODEL_WIDTH * ADAPTER_RANK)
    home_slots = jnp.take(tenant_home, read_tenants, axis=0).astype(jnp.int32)
    tok_blocks = tokens.reshape(device_count, TOK_DEV, MODEL_WIDTH)
    cot_blocks = cotangent.reshape(device_count, TOK_DEV, KV)
    row_blocks = row_tenant.reshape(device_count, TOK_DEV)

    def one_block(storage, block_items):
        tok_block, incoming_gradient_block, row_block, homes_here, read_block = block_items
        fetched_copy = jnp.take(adapters, homes_here, axis=0).astype(jnp.bfloat16)
        down_matrix_rows = fetched_copy[:, :, :MODEL_WIDTH].reshape(READS * ADAPTER_RANK, MODEL_WIDTH)
        up_matrix_rows = fetched_copy[:, :, MODEL_WIDTH:].reshape(READS * ADAPTER_RANK, KV)
        selected_tenants = (row_block[:, None] == read_block[None, :]).astype(jnp.float32)
        selected_tenants = jnp.repeat(selected_tenants, ADAPTER_RANK, axis=1)
        narrow_product = (jnp.dot(tok_block, down_matrix_rows.T, preferred_element_type=jnp.float32) * selected_tenants).astype(jnp.bfloat16)
        frozen_output = jnp.dot(tok_block, value_weight, preferred_element_type=jnp.float32)
        values = (frozen_output + adapter_scale * jnp.dot(narrow_product, up_matrix_rows, preferred_element_type=jnp.float32)).astype(jnp.bfloat16)
        narrow_gradient = (adapter_scale * jnp.dot(incoming_gradient_block, up_matrix_rows.T, preferred_element_type=jnp.float32) * selected_tenants).astype(jnp.bfloat16)
        back_base = jnp.dot(incoming_gradient_block, value_weight.T, preferred_element_type=jnp.float32)
        token_grad = (back_base + jnp.dot(narrow_gradient, down_matrix_rows, preferred_element_type=jnp.float32)).astype(jnp.bfloat16)
        grad_down = jnp.dot(narrow_gradient.T, tok_block, preferred_element_type=jnp.float32)
        up_gradient = adapter_scale * jnp.dot(narrow_product.T, incoming_gradient_block, preferred_element_type=jnp.float32)
        fetched_gradient = jnp.concatenate([grad_down, up_gradient], axis=1).reshape(READS, ADAPTER_RANK, W_AD)
        storage = storage.at[homes_here].add(fetched_gradient)
        return (storage, (values, token_grad))
    empty = jnp.zeros((TENANTS, ADAPTER_RANK, W_AD), jnp.float32)
    position_gradient, outputs = lax.scan(one_block, empty, (tok_blocks, cot_blocks, row_blocks, home_slots, read_tenants))
    values = outputs[0].reshape(ROWS, KV)
    token_grad = outputs[1].reshape(ROWS, MODEL_WIDTH)
    new_first = beta_first * first_moment + (1.0 - beta_first) * position_gradient
    new_second = beta_second * second_moment + (1.0 - beta_second) * position_gradient * position_gradient
    new_adapters = adapters - learn_rate * (new_first / corr_first) / (jnp.sqrt(new_second / corr_second) + adam_eps)
    refreshed = jnp.take(new_adapters, home_slots.reshape(-1), axis=0).astype(jnp.bfloat16)
    return (values, token_grad, new_adapters, new_first, new_second, refreshed)
```

```python
import functools
import math

import jax
import jax.numpy as jnp
from jax import lax
from jax.experimental import pallas as pl
from jax.experimental.pallas import tpu as pltpu
from jax.sharding import PartitionSpec as P

beta_first = 0.9
beta_second = 0.95
learn_rate = 0.1
adam_eps = 1e-08
corr_first = 1.0 - 0.9**10
corr_second = 1.0 - 0.95**10


def bring_back(selected_rows, tenant_total, shard_count, tenants_per_owner):
    adapter_rank_size = selected_rows.shape[1]
    section_width = selected_rows.shape[2]
    received_rows = lax.all_to_all(
        selected_rows, ("tenant", "fsdp"), split_axis=0, concat_axis=0, tiled=True
    )
    received_rows = received_rows.reshape(
        tenant_total, shard_count, tenants_per_owner, adapter_rank_size, section_width
    )
    received_rows = received_rows.transpose(0, 2, 3, 1, 4)
    return received_rows.reshape(
        tenant_total * tenants_per_owner, adapter_rank_size, shard_count * section_width
    )


def per_device(
    tokens,
    cotangent,
    value_weight,
    adapters,
    first_moment,
    second_moment,
    tenant_home,
    read_tenants,
    row_tenant,
):
    tenant_total = lax.axis_size("tenant")
    shard_count = lax.axis_size("fsdp")
    tenant_pos = lax.axis_index("tenant")
    device_pos = tenant_pos * shard_count + lax.axis_index("fsdp")
    position_count = adapters.shape[0]
    adapter_rank_size = adapters.shape[1]
    section_width = adapters.shape[2]
    hidden_width = tokens.shape[1]
    key_value_width = cotangent.shape[1]
    consumer_count = read_tenants.shape[0]
    fetch_count = read_tenants.shape[1]
    tenants_per_owner = fetch_count // tenant_total
    tenant_count = tenant_home.shape[0]
    adapter_scale = 2.0 / math.sqrt(hidden_width * adapter_rank_size)
    matches = read_tenants[:, :, None] == jnp.arange(tenant_count, dtype=jnp.int32)[None, None, :]
    home_slots = jnp.sum(jnp.where(matches, tenant_home[None, None, :], 0), axis=2)
    local_slot = home_slots % position_count
    wanted = lax.dynamic_slice_in_dim(
        local_slot, tenant_pos * tenants_per_owner, tenants_per_owner, 1
    )
    wanted = wanted.reshape(consumer_count * tenants_per_owner)
    selected_rows = jnp.take(adapters, wanted, axis=0).astype(jnp.bfloat16)
    fetched_copy = bring_back(selected_rows, tenant_total, shard_count, tenants_per_owner)
    down_matrix_rows = fetched_copy[:, :, :hidden_width].reshape(
        fetch_count * adapter_rank_size, hidden_width
    )
    up_matrix_rows = fetched_copy[:, :, hidden_width:].reshape(
        fetch_count * adapter_rank_size, key_value_width
    )
    read_block = lax.dynamic_slice_in_dim(read_tenants, device_pos, 1, 0)[0]
    selected_tenants = (row_tenant[:, None] == read_block[None, :]).astype(jnp.float32)
    selected_tenants = jnp.repeat(selected_tenants, adapter_rank_size, axis=1)
    contract_last = (((1,), (1,)), ((), ()))
    contract_first = (((0,), (0,)), ((), ()))
    low_all = lax.dot_general(
        tokens, down_matrix_rows, contract_last, preferred_element_type=jnp.float32
    )
    narrow_product = (low_all * selected_tenants).astype(jnp.bfloat16)
    frozen_output = jnp.dot(
        tokens,
        lax.all_gather(value_weight, "fsdp", axis=0, tiled=True),
        preferred_element_type=jnp.float32,
    )
    values = (
        frozen_output
        + adapter_scale
        * jnp.dot(narrow_product, up_matrix_rows, preferred_element_type=jnp.float32)
    ).astype(jnp.bfloat16)
    narrow_gradient = (
        adapter_scale
        * lax.dot_general(
            cotangent, up_matrix_rows, contract_last, preferred_element_type=jnp.float32
        )
        * selected_tenants
    ).astype(jnp.bfloat16)
    back_base = lax.dot_general(
        cotangent,
        lax.all_gather(value_weight, "fsdp", axis=0, tiled=True),
        contract_last,
        preferred_element_type=jnp.float32,
    )
    token_grad = (
        back_base + jnp.dot(narrow_gradient, down_matrix_rows, preferred_element_type=jnp.float32)
    ).astype(jnp.bfloat16)
    grad_down = lax.dot_general(
        narrow_gradient, tokens, contract_first, preferred_element_type=jnp.float32
    )
    up_gradient = adapter_scale * lax.dot_general(
        narrow_product, cotangent, contract_first, preferred_element_type=jnp.float32
    )
    fetched_gradient = jnp.concatenate([grad_down, up_gradient], axis=1).reshape(
        fetch_count, adapter_rank_size, shard_count * section_width
    )
    departing_rows = fetched_gradient.reshape(
        tenant_total, tenants_per_owner, adapter_rank_size, shard_count, section_width
    ).transpose(0, 3, 1, 2, 4)
    departing_rows = departing_rows.reshape(
        tenant_total * shard_count * tenants_per_owner, adapter_rank_size, section_width
    )
    received_rows = lax.all_to_all(
        departing_rows.astype(jnp.bfloat16),
        ("tenant", "fsdp"),
        split_axis=0,
        concat_axis=0,
        tiled=True,
    ).astype(departing_rows.dtype)
    received_rows = received_rows.reshape(
        consumer_count * tenants_per_owner, adapter_rank_size * section_width
    )
    one_hot = (wanted[:, None] == jnp.arange(position_count, dtype=jnp.int32)[None, :]).astype(
        jnp.float32
    )
    position_gradient = jnp.dot(
        one_hot.T,
        received_rows,
        precision=lax.Precision.HIGHEST,
        preferred_element_type=jnp.float32,
    )
    position_gradient = position_gradient.reshape(position_count, adapter_rank_size, section_width)
    new_first = beta_first * first_moment + (1.0 - beta_first) * position_gradient
    new_second = (
        beta_second * second_moment + (1.0 - beta_second) * position_gradient * position_gradient
    )
    new_adapters = adapters - learn_rate * (new_first / corr_first) / (
        jnp.sqrt(new_second / corr_second) + adam_eps
    )
    fresh_pick = jnp.take(new_adapters, wanted, axis=0).astype(jnp.bfloat16)
    refreshed = bring_back(fresh_pick, tenant_total, shard_count, tenants_per_owner)
    return (values, token_grad, new_adapters, new_first, new_second, refreshed)


MESH = pl.DeviceIdType.MESH


def step_kernel(
    T, F, scale,
    pick, mask, adapters, w_hbm, tok_hbm, cot_hbm, mom1_hbm, mom2_hbm,
    values, tg_hbm, new_ad, new_m1, new_m2, refreshed,
    wbuf, tokens, cot, mom1, mom2, sel, asm, grads, got, acc, low, tgbuf,
    load_sem, ag_send, ag_recv, a2a_send, a2a_recv, tg_sem,
):
    t = lax.axis_index("tenant")
    f = lax.axis_index("fsdp")
    D = T * F
    Z = F // 2
    R = asm.shape[0] // T
    SW = sel.shape[1]
    shard = wbuf.shape[1]
    QR = shard // T
    KV = wbuf.shape[2]
    width = tokens.shape[1]
    me = t * F + f
    z, y = f // 2, f % 2
    oy = 1 - y
    half = T // 2
    tx = (t + half) % T
    tc = t + 1 - 2 * (t % 2)
    qx = tx

    loads = [
        pltpu.make_async_copy(w_hbm, wbuf.at[f], load_sem.at[0]),
        pltpu.make_async_copy(tok_hbm, tokens, load_sem.at[1]),
        pltpu.make_async_copy(cot_hbm, cot, load_sem.at[2]),
        pltpu.make_async_copy(mom1_hbm, mom1, load_sem.at[3]),
        pltpu.make_async_copy(mom2_hbm, mom2, load_sem.at[4]),
    ]
    loads[0].start()
    loads[1].start()
    loads[2].start()
    loads[3].start()
    loads[4].start()
    barrier = pltpu.get_barrier_semaphore()

    def greet(k, carry):
        dev = (me + k) % D
        pl.semaphore_signal(
            barrier, inc=1, device_id=(dev // F, dev % F), device_id_type=MESH
        )
        return carry

    lax.fori_loop(1, D, greet, 0)

    sel[...] = jnp.dot(
        pick[...], adapters[...].astype(jnp.bfloat16), preferred_element_type=jnp.float32
    ).astype(jnp.bfloat16)
    loads[0].wait()
    pl.semaphore_wait(barrier, D - 1)

    def piece(shard_id, q):
        return wbuf.at[shard_id, pl.ds(pl.multiple_of(q * QR, QR), QR)]

    def ag(kind, shard_id, q, dst_t, dst_f):
        return pltpu.make_async_remote_copy(
            src_ref=piece(shard_id, q),
            dst_ref=piece(shard_id, q),
            send_sem=ag_send.at[kind, shard_id],
            recv_sem=ag_recv.at[shard_id, q],
            device_id=(dst_t, dst_f),
            device_id_type=MESH,
        )

    def arrive(shard_id, q):
        pltpu.make_async_copy(
            piece(shard_id, q), piece(shard_id, q), ag_recv.at[shard_id, q]
        ).wait()

    def z_own(act):
        @pl.when(z + 1 < Z)
        def _():
            act(ag(0, f, t, t, f + 2))

        @pl.when(z > 0)
        def _():
            act(ag(1, f, t, t, f - 2))

    def y_own(act):
        act(ag(2, f, t, t, z * 2 + oy))
        act(ag(3, f, qx, t, z * 2 + oy))

    orders = [
        sorted(range(Z), key=lambda s, at=at: (abs(s - at), s if at < Z // 2 else -s))
        for at in range(Z)
    ]

    def near(i):
        pos = 0
        for at in range(Z):
            pos = jnp.where(z == at, orders[at][i], pos)
        return pos

    zz = [z] + [near(i) for i in range(1, Z)]

    def e1(i, act, wait):
        s = zz[i] * 2 + y
        if wait:
            arrive(s, t)

        @pl.when(jnp.logical_and(zz[i] < z, z + 1 < Z))
        def _():
            act(ag(0, s, t, t, f + 2))

        @pl.when(jnp.logical_and(zz[i] > z, z > 0))
        def _():
            act(ag(1, s, t, t, f - 2))

        act(ag(4, s, t, tx, f))
        act(ag(2, s, t, t, z * 2 + oy))
        act(ag(5, s, t, tc, f))

    def e2own(act, wait):
        s = z * 2 + oy
        if wait:
            arrive(s, t)
            arrive(s, qx)
        act(ag(5, s, t, tc, f))
        act(ag(6, s, qx, tc, f))

    def e2(i, act, wait):
        s = zz[i] * 2 + oy
        if wait:
            arrive(s, t)
        act(ag(4, s, t, tx, f))
        act(ag(5, s, t, tc, f))

    def e3(i, yy, act, wait):
        s = zz[i] * 2 + yy
        if wait:
            arrive(s, qx)
        act(ag(6, s, qx, tc, f))

    def start(copy):
        copy.start()

    def sent(copy):
        copy.wait_send()

    def rows(i):
        return pl.ds(pl.multiple_of(i * R, R), R)

    def cols(i):
        return pl.ds(pl.multiple_of(i * SW, SW), SW)

    def spread(n, src_of, dst_at):
        def go(k, carry):
            dev = (me + k) % D
            pltpu.make_async_remote_copy(
                src_ref=src_of(dev),
                dst_ref=dst_at,
                send_sem=a2a_send.at[n, dev],
                recv_sem=a2a_recv.at[n, me],
                device_id=(dev // F, dev % F),
                device_id_type=MESH,
            ).start()
            return carry

        lax.fori_loop(1, D, go, 0)
        pltpu.make_async_copy(src_of(me), dst_at, a2a_recv.at[n, me]).start()

    def collect(n, dst_of):
        def go(k, carry):
            dst = dst_of(k)
            pltpu.make_async_copy(dst, dst, a2a_recv.at[n, k]).wait()
            return carry

        lax.fori_loop(0, D, go, 0)

    def drain(n, src_of):
        def go(k, carry):
            dev = (me + k) % D
            pltpu.make_async_remote_copy(
                src_ref=src_of(dev),
                dst_ref=src_of(dev),
                send_sem=a2a_send.at[n, dev],
                recv_sem=a2a_recv.at[n, me],
                device_id=(dev // F, dev % F),
                device_id_type=MESH,
            ).wait_send()
            return carry

        lax.fori_loop(1, D, go, 0)

    def sel_of(dev):
        return sel.at[rows(dev)]

    def asm_of(dev):
        return asm.at[rows(dev // F), cols(dev % F)]

    def grad_of(dev):
        return grads.at[rows(dev // F), cols(dev % F)]

    def got_of(dev):
        return got.at[rows(dev)]

    def ref_of(dev):
        return refreshed.at[rows(dev // F), cols(dev % F)]

    last = (((1,), (1,)), ((), ()))
    first = (((0,), (0,)), ((), ()))

    def wide(i):
        return pl.ds(pl.multiple_of(i * shard, shard), shard)

    z_own(start)
    y_own(start)
    spread(0, sel_of, asm_of(me))
    for n in range(1, 5):
        loads[n].wait()
    e1(1, start, True)
    e2own(start, True)
    collect(0, asm_of)

    low[...] = jnp.zeros_like(low)

    def lower(k, carry):
        low[...] += lax.dot_general(
            tokens[:, wide(k)], asm[:, wide(k)], last, preferred_element_type=jnp.float32
        )
        return carry

    ups = pl.ds(width, KV)
    narrow_gradient = (
        scale
        * lax.dot_general(cot[...], asm[:, ups], last, preferred_element_type=jnp.float32)
        * mask[...]
    )
    ng = narrow_gradient.astype(jnp.bfloat16)
    ng_t = ng.astype(jnp.float32).T.astype(jnp.bfloat16)

    def gradient(k, carry):
        grads[:, wide(k)] = jnp.dot(
            ng_t, tokens[:, wide(k)], preferred_element_type=jnp.float32
        ).astype(jnp.bfloat16)
        return carry

    lax.fori_loop(0, F, gradient, 0)
    lax.fori_loop(0, F, lower, 0)
    nprod = (low[...] * mask[...]).astype(jnp.bfloat16)
    np_t = nprod.astype(jnp.float32).T.astype(jnp.bfloat16)
    grads[:, ups] = (
        scale * jnp.dot(np_t, cot[...], preferred_element_type=jnp.float32)
    ).astype(jnp.bfloat16)
    spread(1, grad_of, got_of(me))
    if Z > 2:
        e1(2, start, True)
    low[...] = ng.astype(jnp.float32)
    acc[...] = scale * jnp.dot(nprod, asm[:, ups], preferred_element_type=jnp.float32)

    def tg_copy(n, s):
        return pltpu.make_async_copy(
            tgbuf.at[n % 2], tg_hbm.at[:, wide(s)], tg_sem.at[n % 2]
        )

    done = []

    def dots(i, yy):
        s = zz[i] * 2 + yy
        n = len(done)
        if i == 0 and n > 0:
            arrive(s, tc)
            arrive(s, (tc + half) % T)
        elif i > 0:
            arrive(s, tc)
            arrive(s, (tc + half) % T)
        if n >= 2:
            tg_copy(n, done[n - 2]).wait()

        def fwd(k, carry):
            block = pl.ds(pl.multiple_of(k * QR, QR), QR)
            acc[:, block] += jnp.dot(
                tokens[:, wide(s)], wbuf[s, :, block], preferred_element_type=jnp.float32
            )
            return carry

        def bwd(k, carry):
            block = pl.ds(pl.multiple_of(k * QR, QR), QR)
            here = pl.ds(pl.multiple_of(s * shard + k * QR, QR), QR)
            out = lax.dot_general(
                cot[...], wbuf[s, block, :], last, preferred_element_type=jnp.float32
            )
            out += jnp.dot(
                low[...].astype(jnp.bfloat16), asm[:, here],
                preferred_element_type=jnp.float32,
            )
            tgbuf[n % 2, :, block] = out.astype(jnp.bfloat16)
            return carry

        lax.fori_loop(0, KV // QR, fwd, 0)
        lax.fori_loop(0, T, bwd, 0)
        tg_copy(n, s).start()
        done.append(s)

    def update():
        collect(1, got_of)
        g = lax.dot_general(pick[...], got[...], first, preferred_element_type=jnp.float32)
        m1 = beta_first * mom1[...] + (1.0 - beta_first) * g
        m2 = beta_second * mom2[...] + (1.0 - beta_second) * g * g
        new_m1[...] = m1
        new_m2[...] = m2
        na = adapters[...] - learn_rate * (m1 / corr_first) / (
            jnp.sqrt(m2 / corr_second) + adam_eps
        )
        new_ad[...] = na
        drain(0, sel_of)
        sel[...] = jnp.dot(
            pick[...], na.astype(jnp.bfloat16), preferred_element_type=jnp.float32
        ).astype(jnp.bfloat16)
        spread(2, sel_of, ref_of(me))

    dots(0, y)
    e2(1, start, True)
    for i in range(3, Z):
        e1(i, start, True)
    e3(1, y, start, True)
    dots(0, oy)
    for i in range(2, Z):
        e2(i, start, True)
        e3(i - 1, oy, start, True)
        e3(i, y, start, True)
        dots(i - 1, y)
        if i < Z - 1:
            dots(i - 1, oy)
    e3(Z - 1, oy, start, True)
    update()
    dots(Z - 2, oy)
    dots(Z - 1, y)
    dots(Z - 1, oy)
    values[...] = acc[...].astype(jnp.bfloat16)
    collect(2, ref_of)
    for n in (len(done) - 2, len(done) - 1):
        tg_copy(n, done[n]).wait()
    drain(1, grad_of)
    drain(2, sel_of)
    z_own(sent)
    y_own(sent)
    e2own(sent, False)
    for i in range(1, Z):
        e1(i, sent, False)
        e2(i, sent, False)
        e3(i, y, sent, False)
        e3(i, oy, sent, False)


def kernel_device(
    tokens, cotangent, value_weight, adapters, first_moment, second_moment,
    tenant_home, read_tenants, row_tenant,
):
    T = lax.axis_size("tenant")
    F = lax.axis_size("fsdp")
    D = T * F
    tenant_pos = lax.axis_index("tenant")
    device_pos = tenant_pos * F + lax.axis_index("fsdp")
    slots, rank, sw = adapters.shape
    width = tokens.shape[1]
    kv = cotangent.shape[1]
    rows = tokens.shape[0]
    scale = 2.0 / math.sqrt(width * rank)
    tenant_count = tenant_home.shape[0]
    mine = lax.dynamic_slice_in_dim(read_tenants, tenant_pos, 1, 1)[:, 0]
    hits = mine[:, None] == jnp.arange(tenant_count, dtype=jnp.int32)[None, :]
    wanted = jnp.sum(jnp.where(hits, tenant_home[None, :], 0), axis=1) % slots
    left = jnp.arange(D * rank, dtype=jnp.int32)
    right = jnp.arange(slots * rank, dtype=jnp.int32)
    goal = jnp.repeat(wanted, rank) * rank + left % rank
    pick = (goal[:, None] == right[None, :]).astype(jnp.bfloat16)
    read_block = lax.dynamic_slice_in_dim(read_tenants, device_pos, 1, 0)[0]
    mask = row_tenant[:, None] == jnp.repeat(read_block, rank)[None, :]
    mask = mask.astype(jnp.float32)
    flat = (slots * rank, sw)
    f32, bf16 = jnp.float32, jnp.bfloat16
    vmem = pl.BlockSpec(memory_space=pltpu.VMEM)
    hbm = pl.BlockSpec(memory_space=pl.ANY)
    dma = pltpu.SemaphoreType.DMA
    values, token_grad, new_ad, new_m1, new_m2, refreshed = pl.pallas_call(
        functools.partial(step_kernel, T, F, scale),
        out_shape=(
            jax.ShapeDtypeStruct((rows, kv), bf16),
            jax.ShapeDtypeStruct((rows, width), bf16),
            jax.ShapeDtypeStruct(flat, f32),
            jax.ShapeDtypeStruct(flat, f32),
            jax.ShapeDtypeStruct(flat, f32),
            jax.ShapeDtypeStruct((T * rank, F * sw), bf16),
        ),
        in_specs=[vmem, vmem, vmem, hbm, hbm, hbm, hbm, hbm],
        out_specs=(vmem, hbm, vmem, vmem, vmem, vmem),
        scratch_shapes=[
            pltpu.VMEM((F,) + value_weight.shape, bf16),
            pltpu.VMEM(tokens.shape, bf16),
            pltpu.VMEM(cotangent.shape, bf16),
            pltpu.VMEM(flat, f32),
            pltpu.VMEM(flat, f32),
            pltpu.VMEM((D * rank, sw), bf16),
            pltpu.VMEM((T * rank, F * sw), bf16),
            pltpu.VMEM((T * rank, F * sw), bf16),
            pltpu.VMEM((D * rank, sw), bf16),
            pltpu.VMEM((rows, kv), f32),
            pltpu.VMEM((rows, T * rank), f32),
            pltpu.VMEM((2, rows, width // F), bf16),
            dma((5,)),
            dma((7, F)),
            dma((F, T)),
            dma((3, D)),
            dma((3, D)),
            dma((2,)),
        ],
        compiler_params=pltpu.CompilerParams(
            collective_id=0, has_side_effects=True, vmem_limit_bytes=67043328
        ),
    )(
        pick, mask, adapters.reshape(flat), value_weight, tokens, cotangent,
        first_moment.reshape(flat), second_moment.reshape(flat),
    )
    shape = adapters.shape
    return (
        values, token_grad, new_ad.reshape(shape), new_m1.reshape(shape),
        new_m2.reshape(shape), refreshed.reshape(T, rank, F * sw),
    )


def dispatch(*args):
    T = lax.axis_size("tenant")
    F = lax.axis_size("fsdp")
    adapters, read_tenants = args[3], args[7]
    fits = (
        adapters.shape[2] % 128 == 0
        and read_tenants.shape[1] == T
        and T == 4
        and F % 2 == 0
        and F >= 6
    )
    return (kernel_device if fits else per_device)(*args)


def solution(mesh):
    return jax.shard_map(
        dispatch,
        mesh=mesh,
        in_specs=(
            P(("tenant", "fsdp"), None),
            P(("tenant", "fsdp"), None),
            P("fsdp", None),
            P("tenant", None, "fsdp"),
            P("tenant", None, "fsdp"),
            P("tenant", None, "fsdp"),
            P(),
            P(),
            P(("tenant", "fsdp")),
        ),
        out_specs=(
            P(("tenant", "fsdp"), None),
            P(("tenant", "fsdp"), None),
            P("tenant", None, "fsdp"),
            P("tenant", None, "fsdp"),
            P("tenant", None, "fsdp"),
            P(("tenant", "fsdp"), None, None),
        ),
        check_vma=False,
    )
```

```python
import functools
import math

import jax
import jax.numpy as jnp
from jax import lax
from jax.experimental import pallas as pl
from jax.experimental.pallas import tpu as pltpu
from jax.sharding import PartitionSpec as P

beta_first = 0.9
beta_second = 0.95
learn_rate = 0.1
adam_eps = 1e-08
corr_first = 1.0 - 0.9**10
corr_second = 1.0 - 0.95**10


def bring_back(selected_rows, tenant_total, shard_count, tenants_per_owner):
    adapter_rank_size = selected_rows.shape[1]
    section_width = selected_rows.shape[2]
    received_rows = lax.all_to_all(
        selected_rows, ("tenant", "fsdp"), split_axis=0, concat_axis=0, tiled=True
    )
    received_rows = received_rows.reshape(
        tenant_total, shard_count, tenants_per_owner, adapter_rank_size, section_width
    )
    received_rows = received_rows.transpose(0, 2, 3, 1, 4)
    return received_rows.reshape(
        tenant_total * tenants_per_owner, adapter_rank_size, shard_count * section_width
    )


def per_device(
    tokens,
    cotangent,
    value_weight,
    adapters,
    first_moment,
    second_moment,
    tenant_home,
    read_tenants,
    row_tenant,
):
    tenant_total = lax.axis_size("tenant")
    shard_count = lax.axis_size("fsdp")
    tenant_pos = lax.axis_index("tenant")
    device_pos = tenant_pos * shard_count + lax.axis_index("fsdp")
    position_count = adapters.shape[0]
    adapter_rank_size = adapters.shape[1]
    section_width = adapters.shape[2]
    hidden_width = tokens.shape[1]
    key_value_width = cotangent.shape[1]
    consumer_count = read_tenants.shape[0]
    fetch_count = read_tenants.shape[1]
    tenants_per_owner = fetch_count // tenant_total
    tenant_count = tenant_home.shape[0]
    adapter_scale = 2.0 / math.sqrt(hidden_width * adapter_rank_size)
    matches = read_tenants[:, :, None] == jnp.arange(tenant_count, dtype=jnp.int32)[None, None, :]
    home_slots = jnp.sum(jnp.where(matches, tenant_home[None, None, :], 0), axis=2)
    local_slot = home_slots % position_count
    wanted = lax.dynamic_slice_in_dim(
        local_slot, tenant_pos * tenants_per_owner, tenants_per_owner, 1
    )
    wanted = wanted.reshape(consumer_count * tenants_per_owner)
    selected_rows = jnp.take(adapters, wanted, axis=0).astype(jnp.bfloat16)
    fetched_copy = bring_back(selected_rows, tenant_total, shard_count, tenants_per_owner)
    down_matrix_rows = fetched_copy[:, :, :hidden_width].reshape(
        fetch_count * adapter_rank_size, hidden_width
    )
    up_matrix_rows = fetched_copy[:, :, hidden_width:].reshape(
        fetch_count * adapter_rank_size, key_value_width
    )
    read_block = lax.dynamic_slice_in_dim(read_tenants, device_pos, 1, 0)[0]
    selected_tenants = (row_tenant[:, None] == read_block[None, :]).astype(jnp.float32)
    selected_tenants = jnp.repeat(selected_tenants, adapter_rank_size, axis=1)
    contract_last = (((1,), (1,)), ((), ()))
    contract_first = (((0,), (0,)), ((), ()))
    low_all = lax.dot_general(
        tokens, down_matrix_rows, contract_last, preferred_element_type=jnp.float32
    )
    narrow_product = (low_all * selected_tenants).astype(jnp.bfloat16)
    frozen_output = jnp.dot(
        tokens,
        lax.all_gather(value_weight, "fsdp", axis=0, tiled=True),
        preferred_element_type=jnp.float32,
    )
    values = (
        frozen_output
        + adapter_scale
        * jnp.dot(narrow_product, up_matrix_rows, preferred_element_type=jnp.float32)
    ).astype(jnp.bfloat16)
    narrow_gradient = (
        adapter_scale
        * lax.dot_general(
            cotangent, up_matrix_rows, contract_last, preferred_element_type=jnp.float32
        )
        * selected_tenants
    ).astype(jnp.bfloat16)
    back_base = lax.dot_general(
        cotangent,
        lax.all_gather(value_weight, "fsdp", axis=0, tiled=True),
        contract_last,
        preferred_element_type=jnp.float32,
    )
    token_grad = (
        back_base + jnp.dot(narrow_gradient, down_matrix_rows, preferred_element_type=jnp.float32)
    ).astype(jnp.bfloat16)
    grad_down = lax.dot_general(
        narrow_gradient, tokens, contract_first, preferred_element_type=jnp.float32
    )
    up_gradient = adapter_scale * lax.dot_general(
        narrow_product, cotangent, contract_first, preferred_element_type=jnp.float32
    )
    fetched_gradient = jnp.concatenate([grad_down, up_gradient], axis=1).reshape(
        fetch_count, adapter_rank_size, shard_count * section_width
    )
    departing_rows = fetched_gradient.reshape(
        tenant_total, tenants_per_owner, adapter_rank_size, shard_count, section_width
    ).transpose(0, 3, 1, 2, 4)
    departing_rows = departing_rows.reshape(
        tenant_total * shard_count * tenants_per_owner, adapter_rank_size, section_width
    )
    received_rows = lax.all_to_all(
        departing_rows.astype(jnp.bfloat16),
        ("tenant", "fsdp"),
        split_axis=0,
        concat_axis=0,
        tiled=True,
    ).astype(departing_rows.dtype)
    received_rows = received_rows.reshape(
        consumer_count * tenants_per_owner, adapter_rank_size * section_width
    )
    one_hot = (wanted[:, None] == jnp.arange(position_count, dtype=jnp.int32)[None, :]).astype(
        jnp.float32
    )
    position_gradient = jnp.dot(
        one_hot.T,
        received_rows,
        precision=lax.Precision.HIGHEST,
        preferred_element_type=jnp.float32,
    )
    position_gradient = position_gradient.reshape(position_count, adapter_rank_size, section_width)
    new_first = beta_first * first_moment + (1.0 - beta_first) * position_gradient
    new_second = (
        beta_second * second_moment + (1.0 - beta_second) * position_gradient * position_gradient
    )
    new_adapters = adapters - learn_rate * (new_first / corr_first) / (
        jnp.sqrt(new_second / corr_second) + adam_eps
    )
    fresh_pick = jnp.take(new_adapters, wanted, axis=0).astype(jnp.bfloat16)
    refreshed = bring_back(fresh_pick, tenant_total, shard_count, tenants_per_owner)
    return (values, token_grad, new_adapters, new_first, new_second, refreshed)


MESH = pl.DeviceIdType.MESH


def step_kernel(
    T, F, scale,
    pick, mask, adapters, w_hbm, tok_hbm, cot_hbm, mom1_hbm, mom2_hbm,
    values, tg_hbm, slot_grad, refreshed,
    wbuf, tokens, cot, mom1, mom2, sel, asm, grads, got, acc, low, tgbuf,
    load_sem, ag_send, ag_recv, a2a_send, a2a_recv, tg_sem,
):
    t = lax.axis_index("tenant")
    f = lax.axis_index("fsdp")
    D = T * F
    Z = F // 2
    R = asm.shape[0] // T
    SW = sel.shape[1]
    shard = wbuf.shape[1]
    QR = shard // T
    KV = wbuf.shape[2]
    width = tokens.shape[1]
    me = t * F + f
    z, y = f // 2, f % 2
    oy = 1 - y
    half = T // 2
    tx = (t + half) % T
    tc = t + 1 - 2 * (t % 2)
    qx = tx

    loads = [
        pltpu.make_async_copy(w_hbm, wbuf.at[f], load_sem.at[0]),
        pltpu.make_async_copy(tok_hbm, tokens, load_sem.at[1]),
        pltpu.make_async_copy(cot_hbm, cot, load_sem.at[2]),
        pltpu.make_async_copy(mom1_hbm, mom1, load_sem.at[3]),
        pltpu.make_async_copy(mom2_hbm, mom2, load_sem.at[4]),
    ]
    loads[0].start()
    loads[1].start()
    loads[2].start()
    loads[3].start()
    loads[4].start()
    barrier = pltpu.get_barrier_semaphore()

    def greet(k, carry):
        dev = (me + k) % D
        pl.semaphore_signal(
            barrier, inc=1, device_id=(dev // F, dev % F), device_id_type=MESH
        )
        return carry

    lax.fori_loop(1, D, greet, 0)

    sel[...] = jnp.dot(
        pick[...], adapters[...].astype(jnp.bfloat16), preferred_element_type=jnp.float32
    ).astype(jnp.bfloat16)
    loads[0].wait()
    pl.semaphore_wait(barrier, D - 1)

    def piece(shard_id, q):
        return wbuf.at[shard_id, pl.ds(pl.multiple_of(q * QR, QR), QR)]

    def ag(kind, shard_id, q, dst_t, dst_f):
        return pltpu.make_async_remote_copy(
            src_ref=piece(shard_id, q),
            dst_ref=piece(shard_id, q),
            send_sem=ag_send.at[kind, shard_id],
            recv_sem=ag_recv.at[shard_id, q],
            device_id=(dst_t, dst_f),
            device_id_type=MESH,
        )

    def arrive(shard_id, q):
        pltpu.make_async_copy(
            piece(shard_id, q), piece(shard_id, q), ag_recv.at[shard_id, q]
        ).wait()

    def z_own(act):
        @pl.when(z + 1 < Z)
        def _():
            act(ag(0, f, t, t, f + 2))

        @pl.when(z > 0)
        def _():
            act(ag(1, f, t, t, f - 2))

    def y_own(act):
        act(ag(2, f, t, t, z * 2 + oy))

    def y_more(act):
        act(ag(3, f, qx, t, z * 2 + oy))

    orders = [
        sorted(range(Z), key=lambda s, at=at: (abs(s - at), s if at < Z // 2 else -s))
        for at in range(Z)
    ]

    def near(i):
        pos = 0
        for at in range(Z):
            pos = jnp.where(z == at, orders[at][i], pos)
        return pos

    zz = [z] + [near(i) for i in range(1, Z)]

    def e1(i, act, wait):
        s = zz[i] * 2 + y
        if wait:
            arrive(s, t)

        @pl.when(jnp.logical_and(zz[i] < z, z + 1 < Z))
        def _():
            act(ag(0, s, t, t, f + 2))

        @pl.when(jnp.logical_and(zz[i] > z, z > 0))
        def _():
            act(ag(1, s, t, t, f - 2))

        act(ag(4, s, t, tx, f))
        act(ag(2, s, t, t, z * 2 + oy))
        act(ag(5, s, t, tc, f))

    def e2own(act, wait):
        s = z * 2 + oy
        if wait:
            arrive(s, t)
            arrive(s, qx)
        act(ag(5, s, t, tc, f))
        act(ag(6, s, qx, tc, f))

    def e2(i, act, wait):
        s = zz[i] * 2 + oy
        if wait:
            arrive(s, t)
        act(ag(4, s, t, tx, f))
        act(ag(5, s, t, tc, f))

    def e3(i, yy, act, wait):
        s = zz[i] * 2 + yy
        if wait:
            arrive(s, qx)
        act(ag(6, s, qx, tc, f))

    def start(copy):
        copy.start()

    def sent(copy):
        copy.wait_send()

    def rows(i):
        return pl.ds(pl.multiple_of(i * R, R), R)

    def cols(i):
        return pl.ds(pl.multiple_of(i * SW, SW), SW)

    def spread(n, src_of, dst_at):
        def go(k, carry):
            dev = (me + k) % D
            pltpu.make_async_remote_copy(
                src_ref=src_of(dev),
                dst_ref=dst_at,
                send_sem=a2a_send.at[n, dev],
                recv_sem=a2a_recv.at[n, me],
                device_id=(dev // F, dev % F),
                device_id_type=MESH,
            ).start()
            return carry

        lax.fori_loop(1, D, go, 0)
        pltpu.make_async_copy(src_of(me), dst_at, a2a_recv.at[n, me]).start()

    def collect(n, dst_of):
        def go(k, carry):
            dst = dst_of(k)
            pltpu.make_async_copy(dst, dst, a2a_recv.at[n, k]).wait()
            return carry

        lax.fori_loop(0, D, go, 0)

    def drain(n, src_of):
        def go(k, carry):
            dev = (me + k) % D
            pltpu.make_async_remote_copy(
                src_ref=src_of(dev),
                dst_ref=src_of(dev),
                send_sem=a2a_send.at[n, dev],
                recv_sem=a2a_recv.at[n, me],
                device_id=(dev // F, dev % F),
                device_id_type=MESH,
            ).wait_send()
            return carry

        lax.fori_loop(1, D, go, 0)

    def sel_of(dev):
        return sel.at[rows(dev)]

    def asm_of(dev):
        return asm.at[rows(dev // F), cols(dev % F)]

    def grad_of(dev):
        return grads.at[rows(dev // F), cols(dev % F)]

    def got_of(dev):
        return got.at[rows(dev)]

    def ref_of(dev):
        return refreshed.at[rows(dev // F), cols(dev % F)]

    last = (((1,), (1,)), ((), ()))
    first = (((0,), (0,)), ((), ()))

    def wide(i):
        return pl.ds(pl.multiple_of(i * shard, shard), shard)

    z_own(start)
    y_own(start)
    for n in range(1, 5):
        loads[n].wait()
    e1(1, start, True)
    spread(0, sel_of, asm_of(me))
    y_more(start)
    e1(2, start, True)
    e2own(start, True)
    e2(1, start, True)
    for i in range(3, Z):
        e1(i, start, True)
    collect(0, asm_of)

    low[...] = jnp.zeros_like(low)

    def lower(k, carry):
        low[...] += lax.dot_general(
            tokens[:, wide(k)], asm[:, wide(k)], last, preferred_element_type=jnp.float32
        )
        return carry

    ups = pl.ds(width, KV)
    narrow_gradient = (
        scale
        * lax.dot_general(cot[...], asm[:, ups], last, preferred_element_type=jnp.float32)
        * mask[...]
    )
    ng = narrow_gradient.astype(jnp.bfloat16)
    ng_t = ng.astype(jnp.float32).T.astype(jnp.bfloat16)

    def gradient(k, carry):
        grads[:, wide(k)] = jnp.dot(
            ng_t, tokens[:, wide(k)], preferred_element_type=jnp.float32
        ).astype(jnp.bfloat16)
        return carry

    lax.fori_loop(0, F, gradient, 0)
    lax.fori_loop(0, F, lower, 0)
    nprod = (low[...] * mask[...]).astype(jnp.bfloat16)
    np_t = nprod.astype(jnp.float32).T.astype(jnp.bfloat16)
    grads[:, ups] = (
        scale * jnp.dot(np_t, cot[...], preferred_element_type=jnp.float32)
    ).astype(jnp.bfloat16)
    spread(1, grad_of, got_of(me))
    low[...] = ng.astype(jnp.float32)
    acc[...] = scale * jnp.dot(nprod, asm[:, ups], preferred_element_type=jnp.float32)

    def tg_copy(n, s):
        return pltpu.make_async_copy(
            tgbuf.at[n % 2], tg_hbm.at[:, wide(s)], tg_sem.at[n % 2]
        )

    done = []

    def dots(i, yy):
        s = zz[i] * 2 + yy
        n = len(done)
        if i == 0 and n > 0:
            arrive(s, tc)
            arrive(s, (tc + half) % T)
        elif i > 0:
            arrive(s, tc)
            arrive(s, (tc + half) % T)
        if n >= 2:
            tg_copy(n, done[n - 2]).wait()

        def fwd(k, carry):
            block = pl.ds(pl.multiple_of(k * QR, QR), QR)
            acc[:, block] += jnp.dot(
                tokens[:, wide(s)], wbuf[s, :, block], preferred_element_type=jnp.float32
            )
            return carry

        def bwd(k, carry):
            block = pl.ds(pl.multiple_of(k * QR, QR), QR)
            here = pl.ds(pl.multiple_of(s * shard + k * QR, QR), QR)
            out = lax.dot_general(
                cot[...], wbuf[s, block, :], last, preferred_element_type=jnp.float32
            )
            out += jnp.dot(
                low[...].astype(jnp.bfloat16), asm[:, here],
                preferred_element_type=jnp.float32,
            )
            tgbuf[n % 2, :, block] = out.astype(jnp.bfloat16)
            return carry

        lax.fori_loop(0, KV // QR, fwd, 0)
        lax.fori_loop(0, T, bwd, 0)
        tg_copy(n, s).start()
        done.append(s)

    def update():
        collect(1, got_of)
        g = lax.dot_general(pick[...], got[...], first, preferred_element_type=jnp.float32)
        m1 = beta_first * mom1[...] + (1.0 - beta_first) * g
        m2 = beta_second * mom2[...] + (1.0 - beta_second) * g * g
        na = adapters[...] - learn_rate * (m1 / corr_first) / (
            jnp.sqrt(m2 / corr_second) + adam_eps
        )
        slot_grad[...] = g
        drain(0, sel_of)
        sel[...] = jnp.dot(
            pick[...], na.astype(jnp.bfloat16), preferred_element_type=jnp.float32
        ).astype(jnp.bfloat16)
        spread(2, sel_of, ref_of(me))

    dots(0, y)
    e3(1, y, start, True)
    dots(0, oy)
    for i in range(2, Z):
        e2(i, start, True)
        e3(i - 1, oy, start, True)
        e3(i, y, start, True)
        dots(i - 1, y)
        if i < Z - 1:
            dots(i - 1, oy)
    e3(Z - 1, oy, start, True)
    update()
    dots(Z - 2, oy)
    dots(Z - 1, y)
    dots(Z - 1, oy)
    values[...] = acc[...].astype(jnp.bfloat16)
    collect(2, ref_of)
    for n in (len(done) - 2, len(done) - 1):
        tg_copy(n, done[n]).wait()
    drain(1, grad_of)
    drain(2, sel_of)
    z_own(sent)
    y_own(sent)
    y_more(sent)
    e2own(sent, False)
    for i in range(1, Z):
        e1(i, sent, False)
        e2(i, sent, False)
        e3(i, y, sent, False)
        e3(i, oy, sent, False)


def kernel_device(
    tokens, cotangent, value_weight, adapters, first_moment, second_moment,
    tenant_home, read_tenants, row_tenant,
):
    T = lax.axis_size("tenant")
    F = lax.axis_size("fsdp")
    D = T * F
    tenant_pos = lax.axis_index("tenant")
    device_pos = tenant_pos * F + lax.axis_index("fsdp")
    slots, rank, sw = adapters.shape
    width = tokens.shape[1]
    kv = cotangent.shape[1]
    rows = tokens.shape[0]
    scale = 2.0 / math.sqrt(width * rank)
    tenant_count = tenant_home.shape[0]
    mine = lax.dynamic_slice_in_dim(read_tenants, tenant_pos, 1, 1)[:, 0]
    hits = mine[:, None] == jnp.arange(tenant_count, dtype=jnp.int32)[None, :]
    wanted = jnp.sum(jnp.where(hits, tenant_home[None, :], 0), axis=1) % slots
    left = jnp.arange(D * rank, dtype=jnp.int32)
    right = jnp.arange(slots * rank, dtype=jnp.int32)
    goal = jnp.repeat(wanted, rank) * rank + left % rank
    pick = (goal[:, None] == right[None, :]).astype(jnp.bfloat16)
    read_block = lax.dynamic_slice_in_dim(read_tenants, device_pos, 1, 0)[0]
    mask = row_tenant[:, None] == jnp.repeat(read_block, rank)[None, :]
    mask = mask.astype(jnp.float32)
    flat = (slots * rank, sw)
    f32, bf16 = jnp.float32, jnp.bfloat16
    vmem = pl.BlockSpec(memory_space=pltpu.VMEM)
    hbm = pl.BlockSpec(memory_space=pl.ANY)
    dma = pltpu.SemaphoreType.DMA
    values, token_grad, g, refreshed = pl.pallas_call(
        functools.partial(step_kernel, T, F, scale),
        out_shape=(
            jax.ShapeDtypeStruct((rows, kv), bf16),
            jax.ShapeDtypeStruct((rows, width), bf16),
            jax.ShapeDtypeStruct(flat, f32),
            jax.ShapeDtypeStruct((T * rank, F * sw), bf16),
        ),
        in_specs=[vmem, vmem, vmem, hbm, hbm, hbm, hbm, hbm],
        out_specs=(vmem, hbm, vmem, vmem),
        scratch_shapes=[
            pltpu.VMEM((F,) + value_weight.shape, bf16),
            pltpu.VMEM(tokens.shape, bf16),
            pltpu.VMEM(cotangent.shape, bf16),
            pltpu.VMEM(flat, f32),
            pltpu.VMEM(flat, f32),
            pltpu.VMEM((D * rank, sw), bf16),
            pltpu.VMEM((T * rank, F * sw), bf16),
            pltpu.VMEM((T * rank, F * sw), bf16),
            pltpu.VMEM((D * rank, sw), bf16),
            pltpu.VMEM((rows, kv), f32),
            pltpu.VMEM((rows, T * rank), f32),
            pltpu.VMEM((2, rows, width // F), bf16),
            dma((5,)),
            dma((7, F)),
            dma((F, T)),
            dma((3, D)),
            dma((3, D)),
            dma((2,)),
        ],
        compiler_params=pltpu.CompilerParams(
            collective_id=0, has_side_effects=True, vmem_limit_bytes=67043328
        ),
    )(
        pick, mask, adapters.reshape(flat), value_weight, tokens, cotangent,
        first_moment.reshape(flat), second_moment.reshape(flat),
    )
    g = g.reshape(adapters.shape)
    new_m1 = beta_first * first_moment + (1.0 - beta_first) * g
    new_m2 = beta_second * second_moment + (1.0 - beta_second) * g * g
    new_ad = adapters - learn_rate * (new_m1 / corr_first) / (
        jnp.sqrt(new_m2 / corr_second) + adam_eps
    )
    return (
        values, token_grad, new_ad, new_m1, new_m2,
        refreshed.reshape(T, rank, F * sw),
    )


def dispatch(*args):
    T = lax.axis_size("tenant")
    F = lax.axis_size("fsdp")
    adapters, read_tenants = args[3], args[7]
    fits = (
        adapters.shape[2] % 128 == 0
        and read_tenants.shape[1] == T
        and T == 4
        and F % 2 == 0
        and F >= 6
    )
    return (kernel_device if fits else per_device)(*args)


def solution(mesh):
    return jax.shard_map(
        dispatch,
        mesh=mesh,
        in_specs=(
            P(("tenant", "fsdp"), None),
            P(("tenant", "fsdp"), None),
            P("fsdp", None),
            P("tenant", None, "fsdp"),
            P("tenant", None, "fsdp"),
            P("tenant", None, "fsdp"),
            P(),
            P(),
            P(("tenant", "fsdp")),
        ),
        out_specs=(
            P(("tenant", "fsdp"), None),
            P(("tenant", "fsdp"), None),
            P("tenant", None, "fsdp"),
            P("tenant", None, "fsdp"),
            P("tenant", None, "fsdp"),
            P(("tenant", "fsdp"), None, None),
        ),
        check_vma=False,
    )
```
